32 devices in a mesh: dir: 4 (over x, core), tb: 8 (over z, y).
Axes of the slice: x: 2, y: 2, z: 4, core: 2. Of those that a mesh axis runs over, the one named last changes fastest.
Arguments:
- visibilities: bfloat16 [8192, 128], P('tb'), may hold values from -6 to 6
- uv_coords: bfloat16 [2, 8192], P(None, 'tb'), may hold values from -32 to 32
- comp_lm: float32 [2, 12288], P(None, 'dir'), may hold values from -0.25 to 0.25
- spectra: bfloat16 [2, 12288, 128], P(None, 'dir'), may hold values from -0.1875 to 0.1875
- ridge_weight: float32 [128], replicated, may hold values from 32 to 512
- assignment: int32 [12288], P('dir'), may hold values from 0 to 3071, as said below
- peel_order: int32 [12], P('dir'), may hold values from 0 to 2, as said below
- block_tile: int32 [256, 1], P('tb'), may hold values from 0 to 7; in each aligned block of 32 rows (0 to 31, 32 to 63, ...) at most 8 rows name the same one
Outputs:
- residual: bfloat16 [8192, 128], P('tb')
- subgrids: float32 [8, 2, 1024, 128], P('tb', None, 'dir')
The draws below stay inside these ranges and needn't reach their ends.
Inputs may be any that keep to these rules, and one draw needn't show every extreme that they name: `assignment`: each owner's 3 * 1024 entries are a permutation of its local component numbers. `peel_order`: each owner's 3 entries are a permutation of its directions. `block_tile`: among the 32 blocks of one index of tb no tile is named more than 8 times; every tile is named by some block of the whole array.
All inputs are finite; a program needn't handle non-finite values.
Results may differ from the reference program's by a relative error of at most 0.0064.
Values may be sent and summed in bfloat16 or wider, within the bound.
A program may use at most 64 MiB of HBM per device.

```python
import math
import jax
import jax.numpy as jnp
import numpy as np
from jax import lax

COLS = 128
NCOMP = 1024
GRID = 32
DIR_DEV = 3
ITERS = 4
BB = 32
GB = 128
ROWS_DEV = 1024
NB = 32
MOST = 8
SAMPLES = 8192
BLOCKS = 256
TILES = 8
NPOOL = 12288
PIX = 1024
N_DIR = 4


def shuffle_pool(subkey):
    return jax.random.permutation(subkey, DIR_DEV * NCOMP)


def shuffle_order(subkey):
    return jax.random.permutation(subkey, DIR_DEV)


def draw_assignment(key, part):
    subkeys = jax.random.split(jax.random.fold_in(key, 11), N_DIR)
    permuted = jax.vmap(shuffle_pool)(subkeys)
    return permuted.reshape(-1).astype(jnp.int32)


def draw_peel_order(key, part):
    subkeys = jax.random.split(jax.random.fold_in(key, 23), N_DIR)
    permuted = jax.vmap(shuffle_order)(subkeys)
    return permuted.reshape(-1).astype(jnp.int32)


def shard_levels(own_key, dims, cuts, low, largest):
    loudness = 1.0
    for dim, blocks in cuts:
        steps = jax.random.uniform(jax.random.fold_in(jax.random.fold_in(own_key, 6), dim), (blocks,), jnp.float32, low / len(cuts), largest / len(cuts))
        loudness = loudness * jnp.repeat(jnp.exp(steps), dims[dim] // blocks).reshape((-1,) + (1,) * (len(dims) - 1 - dim))
    return loudness


def deal_out(rng, own, number, rows, amount, top, reach, lean):
    ranking = jax.random.permutation(rng, amount)
    crowded, common = portions_of(amount, rows * top, reach, lean, True), portions_of(amount, rows * top, reach, lean, False)
    places = jnp.arange(amount)

    def named(tallies, offset_by):
        used = int((tallies > 0).sum())
        fixed = max(1, used // 4)
        shifted = fixed + (places - fixed + offset_by * (used - fixed)) % max(1, amount - fixed)
        return jnp.zeros((amount,), jnp.int32).at[ranking[jnp.where(places < fixed, places, shifted)]].set(jnp.asarray(tallies, jnp.int32))

    tallies = jnp.where(number % 4 == 0, named(crowded, number // 4), named(common, number - number // 4 - 1))
    mixed = jax.random.permutation(jax.random.fold_in(own, 3), amount)
    donor, receiver = mixed[0:amount // 2 * 2:2], mixed[1:amount // 2 * 2:2]
    room = jnp.minimum(tallies[donor] - 1, reach - tallies[receiver]) // 2
    room = jnp.where((donor == ranking[0]) | (receiver == ranking[0]) | (tallies[receiver] == 0), 0, jnp.maximum(room, 0))
    shifted = jax.random.randint(jax.random.fold_in(own, 4), (amount // 2,), 0, 1 << 20) % (room + 1)
    tallies = tallies.at[donor].add(-shifted).at[receiver].add(shifted)
    labels = jnp.searchsorted(jnp.cumsum(tallies), jnp.arange(rows * top), side="right").astype(jnp.int32)
    listing = labels.reshape(top, rows).T
    listing = listing[jax.random.permutation(jax.random.fold_in(own, 1), rows)]
    offset_by = jax.random.randint(jax.random.fold_in(own, 2), (rows, 1), 0, top)
    return jnp.take_along_axis(listing, (jnp.arange(top)[None, :] + offset_by) % top, axis=1)


def portions_of(number_of, total, bound, lean, full):
    loads = [(1 << 20) // math.isqrt(grade ** lean) + 1 for grade in range(1, number_of + 1)]
    largest = bound if full else min(bound, max(-(-total // number_of), total * loads[0] // sum(loads)))
    least = 1 if total - largest >= number_of - 1 else 0
    given, surplus = [largest] + [least] * (number_of - 1), total - largest - least * (number_of - 1)
    while surplus > 0:
        candidates = [i for i in range(1, number_of) if given[i] < largest] or [i for i in range(1, number_of) if given[i] < bound]
        pool, remaining = sum([loads[i] for i in candidates]), surplus
        for i in candidates:
            more = min(bound - given[i], max(1, remaining * loads[i] // pool), surplus)
            given[i] = given[i] + more
            surplus = surplus - more
    return np.array(given)


def bell_draw(key, dims, scale, most, cuts=(), held_as=jnp.bfloat16):
    loudness = shard_levels(key, dims, cuts, -0.22, 0.18) if cuts else 1.0
    result = jax.random.normal(key, dims, jnp.float32) * scale * loudness
    return jnp.minimum(jnp.maximum(result, -most), most).astype(held_as)


def setup_inputs(seed: int = 0) -> dict:
    arg_keys = jax.random.split(jax.random.key(seed), 9)
    visibilities = bell_draw(arg_keys[0], (SAMPLES, COLS), 1.0, 6.0, ((0, 8),))
    uv_coords = jnp.clip(jax.random.uniform(arg_keys[1], (2, SAMPLES), jnp.float32, -32.0, 32.0) * shard_levels(arg_keys[1], (2, SAMPLES), ((1, 8),), -0.4, 0.0), -32.0, 32.0).astype(jnp.bfloat16)
    comp_lm = jnp.clip(jax.random.uniform(arg_keys[2], (2, NPOOL), jnp.float32, -0.25, 0.25) * shard_levels(arg_keys[2], (2, NPOOL), ((1, 4),), -0.4, 0.0), -0.25, 0.25)
    spectra = bell_draw(arg_keys[3], (2, NPOOL, COLS), NCOMP ** -0.5, 0.1875, ((1, 4),))
    ridge_weight = jnp.clip(jnp.exp(jax.random.uniform(arg_keys[4], (COLS,), jnp.float32, math.log(32.0), math.log(512.0))), 32.0, 512.0)
    assignment = draw_assignment(jax.random.fold_in(arg_keys[8], 71), 0)
    peel_order = draw_peel_order(jax.random.fold_in(arg_keys[8], 71), 0)
    block_tile_keys = jax.random.split(jax.random.fold_in(arg_keys[7], 1), BLOCKS // NB)
    block_tile_turns = jax.random.permutation(jax.random.fold_in(arg_keys[7], 3), BLOCKS // NB)
    block_tile = jax.vmap(lambda own, number: deal_out(jax.random.fold_in(arg_keys[7], 2), own, number, NB, TILES, 1, MOST, 2))(block_tile_keys, block_tile_turns).reshape((BLOCKS, 1))
    return {"visibilities": visibilities, "uv_coords": uv_coords, "comp_lm": comp_lm, "spectra": spectra, "ridge_weight": ridge_weight, "assignment": assignment, "peel_order": peel_order, "block_tile": block_tile}


TWO_PI = 2.0 * math.pi


def phase_table(coords, lm_dir):
    phases = TWO_PI * (coords[0][:, None] * lm_dir[0][None, :] + coords[1][:, None] * lm_dir[1][None, :])
    return jnp.concatenate([jnp.cos(phases), jnp.sin(phases)], axis=1).astype(jnp.bfloat16)


def predict(coords, lm_dir, spec_dir):
    phase_rows = phase_table(coords, lm_dir)
    return jnp.dot(phase_rows, spec_dir.reshape(-1, spec_dir.shape[-1]), preferred_element_type=jnp.float32)


def neighbours(gain_values):
    blocks, columns = gain_values.shape
    paired = gain_values.reshape(blocks, columns // 2, 2)
    padded = jnp.pad(paired, ((0, 0), (1, 1), (0, 0)), mode="edge")
    return (0.5 * (padded[:, :-2] + padded[:, 2:])).reshape(blocks, columns)


def fit_subtract(remains, model_rows, ridge_weight):
    blocks = remains.shape[0] // GB
    res_blocks = remains.reshape(blocks, GB, -1)
    mod_blocks = model_rows.reshape(blocks, GB, -1)
    cross_sum = jnp.sum(res_blocks * mod_blocks, axis=1)
    power_sum = jnp.sum(mod_blocks * mod_blocks, axis=1)
    gain_values = jnp.ones_like(cross_sum)
    for sweep_index in range(ITERS):
        gain_values = (cross_sum + ridge_weight * neighbours(gain_values)) / (power_sum + ridge_weight)
    return (res_blocks - gain_values[:, None, :] * mod_blocks).reshape(remains.shape)


def grid_table(coords, x_pixel, y_pixel):
    phases = TWO_PI * (coords[0][:, None] * x_pixel[None, :] + coords[1][:, None] * y_pixel[None, :]) / (2.0 * GRID)
    return jnp.cos(phases).astype(jnp.bfloat16), jnp.sin(phases).astype(jnp.bfloat16)


def reference(visibilities, uv_coords, comp_lm, spectra, ridge_weight, assignment, peel_order, block_tile):
    columns = visibilities.shape[1]
    ndirs = peel_order.shape[0]
    pool_owner = DIR_DEV * NCOMP
    groups = visibilities.shape[0] // ROWS_DEV

    def one_group(group_index):
        first_row = group_index * ROWS_DEV
        remains = lax.dynamic_slice_in_dim(visibilities, first_row, ROWS_DEV, 0).astype(jnp.float32)
        coords = lax.dynamic_slice_in_dim(uv_coords, first_row, ROWS_DEV, 1).astype(jnp.float32)
        rounded = remains.astype(jnp.bfloat16)
        for position in range(ndirs):
            owner_base = (position // DIR_DEV) * pool_owner
            first_entry = owner_base + peel_order[position] * NCOMP
            chosen = owner_base + lax.dynamic_slice_in_dim(assignment, first_entry, NCOMP, 0)
            model_rows = predict(coords, comp_lm[:, chosen], spectra[:, chosen])
            remains = fit_subtract(remains, model_rows, ridge_weight)
            if (position + 1) % DIR_DEV == 0:
                rounded = lax.optimization_barrier(remains.astype(jnp.bfloat16))
                remains = rounded.astype(jnp.float32)
        return rounded

    residual = lax.map(one_group, jnp.arange(groups, dtype=jnp.int32)).reshape(-1, columns)
    pixels = jnp.arange(PIX, dtype=jnp.int32)
    x_pixel = (pixels // GRID - GRID // 2).astype(jnp.float32)
    y_pixel = (pixels % GRID - GRID // 2).astype(jnp.float32)
    blocks = residual.reshape(-1, BB, columns)
    block_coords = uv_coords.astype(jnp.float32).reshape(2, -1, BB).transpose(1, 0, 2)
    contract = (((0,), (0,)), ((), ()))

    def add_block(subgrids, block_items):
        block_rows, coords, tile_index = block_items
        cos_table, sin_table = grid_table(coords, x_pixel, y_pixel)
        real_part = lax.dot_general(cos_table, block_rows, contract, preferred_element_type=jnp.float32)
        imag_part = lax.dot_general(sin_table, block_rows, contract, preferred_element_type=jnp.float32)
        update = jnp.stack([real_part, imag_part])
        return subgrids.at[tile_index].add(update), None

    initial = jnp.zeros((TILES, 2, PIX, columns), jnp.float32)
    subgrids, unused = lax.scan(add_block, initial, (blocks, block_coords, block_tile[:, 0]))
    return residual, subgrids * (float(ROWS_DEV) ** -0.5)
```

```python
import functools
import math

import jax
import jax.numpy as jnp
from jax import lax
from jax.experimental import pallas as pl
from jax.experimental.pallas import tpu as pltpu
from jax.sharding import PartitionSpec as P

NCOMP = 1024
GRID = 32
DIR_DEV = 3
ITERS = 4
BB = 32
GB = 128
ROWS_DEV = 1024
PIX = 1024

MESH = pl.DeviceIdType.MESH
F32 = jnp.float32
BF16 = jnp.bfloat16
LANES = 128
CHUNK = 512
SUB = 32

SIN_FIT = (
    4.442882919124344,
    -7.308245686509099,
    3.6063542184331383,
    -0.8461116503741475,
    0.10982451642439378,
)
COS_FIT = (
    1.4142134962552289,
    -6.978850948563853,
    5.7394603769076955,
    -1.8835579059892091,
    0.31068802753070307,
)


def horner(square, fit):
    total = fit[-1]
    for coefficient in fit[-2::-1]:
        total = total * square + coefficient
    return total


def turn_cos_sin(turns):
    part = turns - jnp.round(turns)
    square = part * part
    half_sin = part * horner(square, SIN_FIT)
    half_cos = horner(square, COS_FIT)
    return (1.0 - half_sin * half_sin).astype(BF16), (half_sin * half_cos).astype(BF16)


def kernel(
    owners,
    peers,
    slots,
    vis_ref,
    coord_ref,
    lm_ref,
    spec_ref,
    ridge_ref,
    entry_ref,
    block_of_ref,
    sendc_ref,
    resid_ref,
    grid_ref,
    masked,
    turned_a,
    turned_b,
    acc,
    models_out,
    models_in,
    resid,
    rows_out,
    rows_in,
    coords_in,
    tables,
    m_send,
    m_recv,
    r_send,
    r_recv,
    d_send,
    d_recv,
    c_send,
    c_recv,
):
    me_d = lax.axis_index("dir")
    me_t = lax.axis_index("tb")
    sample_rows, columns = vis_ref.shape
    comps = lm_ref.shape[1]
    group_rows = sample_rows // owners
    block_count = sample_rows // BB
    group_blocks = block_count // owners
    slot_rows = slots * BB

    barrier = pltpu.get_barrier_semaphore()
    for k in range(1, owners):
        pl.semaphore_signal(
            barrier, inc=1, device_id={"dir": lax.rem(me_d + k, owners)}, device_id_type=MESH
        )

    def greet(k, carry):
        pl.semaphore_signal(
            barrier, inc=1, device_id={"tb": lax.rem(me_t + k, peers)}, device_id_type=MESH
        )
        return carry

    lax.fori_loop(1, peers, greet, 0)
    pl.semaphore_wait(barrier, owners - 1 + peers - 1)

    def coords_copy(src, dst, sem, to):
        return pltpu.make_async_remote_copy(
            src_ref=sendc_ref.at[src],
            dst_ref=coords_in.at[dst],
            send_sem=c_send.at[src],
            recv_sem=c_recv.at[sem],
            device_id={"tb": to},
            device_id_type=MESH,
        )

    def send_coords(k, carry):
        to = lax.rem(me_t + k, peers)
        coords_copy(to, me_t, me_t, to).start()
        return carry

    lax.fori_loop(1, peers, send_coords, 0)
    coords_in[pl.ds(me_t, 1)] = sendc_ref[pl.ds(me_t, 1)]

    strips = comps // LANES
    padded = -(-strips // 16) * 16
    named = entry_ref[0:1, :]
    place = entry_ref[1:2, :].astype(F32)
    low = lax.broadcasted_iota(jnp.int32, (LANES, comps), 0)
    high = lax.broadcasted_iota(jnp.int32, (padded, comps), 0)
    at_low = jnp.where(low == named % LANES, 1.0, 0.0).astype(BF16)
    at_high = jnp.where(high == named // LANES, place, 0.0).astype(BF16)
    positions = lax.dot_general(
        at_low, at_high, (((1,), (1,)), ((), ())), preferred_element_type=F32
    )
    for strip in range(strips):
        own = jnp.broadcast_to(positions[:, strip : strip + 1], (LANES, columns))
        span = pl.ds(strip * LANES, LANES)
        for part in range(2):
            values = spec_ref[part, span, :].astype(F32)
            for position in range(DIR_DEV):
                masked[part, span, position * columns : (position + 1) * columns] = jnp.where(
                    own == float(position), values, 0.0
                ).astype(BF16)

    def models_copy(group, owner, to):
        return pltpu.make_async_remote_copy(
            src_ref=models_out.at[group],
            dst_ref=models_in.at[owner],
            send_sem=m_send.at[group],
            recv_sem=m_recv.at[owner],
            device_id={"dir": to},
            device_id_type=MESH,
        )

    def predict_group(k, carry):
        group = lax.rem(me_d + k, owners)
        first = group * group_rows
        for chunk in range(comps // CHUNK):
            turned = turned_a if chunk % 2 == 0 else turned_b
            span = slice(chunk * CHUNK, (chunk + 1) * CHUNK)
            l_row = lm_ref[0:1, span]
            m_row = lm_ref[1:2, span]
            for sub in range(group_rows // SUB):
                coord = coord_ref[pl.ds(pl.multiple_of(first + sub * SUB, SUB), SUB), :]
                cos_part, sin_part = turn_cos_sin(coord[:, 0:1] * l_row + coord[:, 1:2] * m_row)
                turned[0, sub * SUB : (sub + 1) * SUB, :] = cos_part
                turned[1, sub * SUB : (sub + 1) * SUB, :] = sin_part
            update = jnp.dot(turned[0], masked[0, span, :], preferred_element_type=F32) + jnp.dot(
                turned[1], masked[1, span, :], preferred_element_type=F32
            )
            if chunk == 0:
                acc[...] = update
            elif chunk < comps // CHUNK - 1:
                acc[...] += update
            else:
                final = (acc[...] + update).astype(BF16)

        @pl.when(k < owners)
        def _():
            models_out[group] = final
            models_copy(group, me_d, group).start()

        @pl.when(k == owners)
        def _():
            models_in[me_d] = final

        return carry

    lax.fori_loop(1, owners + 1, predict_group, 0)

    def wait_coords(k, carry):
        source = lax.rem(me_t + k, peers)
        coords_copy(source, source, source, source).wait()
        return carry

    lax.fori_loop(1, peers, wait_coords, 0)
    share = grid_ref.shape[1]
    pixel = me_d * share + lax.broadcasted_iota(jnp.int32, (share, 16), 0)
    which = lax.broadcasted_iota(jnp.int32, (share, 16), 1)
    pixel_xy = jnp.where(
        which == 0,
        (pixel // GRID - GRID // 2).astype(F32),
        jnp.where(which == 1, (pixel % GRID - GRID // 2).astype(F32), 0.0),
    )
    pixel_xy = (pixel_xy / (2.0 * GRID)).astype(BF16)

    def make_table(source, carry):
        turns = jnp.dot(pixel_xy, coords_in[source], preferred_element_type=F32)
        cos_part, sin_part = turn_cos_sin(turns)
        tables[source, 0:share, :] = cos_part
        tables[source, share : 2 * share, :] = sin_part
        return carry

    lax.fori_loop(0, peers, make_table, 0)

    def wait_models(k, carry):
        source = lax.rem(me_d + k, owners)
        models_copy(source, source, source).wait()
        return carry

    lax.fori_loop(1, owners, wait_models, 0)

    gain_blocks = group_rows // GB
    first = me_d * group_rows
    ridge = jnp.broadcast_to(ridge_ref[...], (8, columns))
    lane = lax.broadcasted_iota(jnp.int32, (8, columns), 1)

    def over_rows(value):
        total = jnp.sum(jnp.sum(value, axis=0), axis=0, keepdims=True)
        return jnp.broadcast_to(total, (8, columns))

    def peel_owner(owner, remains):
        out = []
        for block in range(gain_blocks):
            rest = remains[block]
            for position in range(DIR_DEV):
                model = models_in[
                    owner,
                    block * GB : (block + 1) * GB,
                    position * columns : (position + 1) * columns,
                ].astype(F32)
                model = model.reshape(GB // 8, 8, columns)
                cross_sum = over_rows(rest * model)
                inverse = 1.0 / (over_rows(model * model) + ridge)
                gain = jnp.ones_like(cross_sum)
                for sweep in range(ITERS):
                    before = jnp.where(lane < 2, gain, pltpu.roll(gain, 2, 1))
                    after = jnp.where(
                        lane >= columns - 2, gain, pltpu.roll(gain, columns - 2, 1)
                    )
                    gain = (cross_sum + ridge * (0.5 * (before + after))) * inverse
                rest = rest - gain[None] * model
            out.append(rest.astype(BF16).astype(F32))
        return tuple(out)

    start = tuple(
        vis_ref[pl.ds(pl.multiple_of(first + block * GB, GB), GB), :]
        .astype(F32)
        .reshape(GB // 8, 8, columns)
        for block in range(gain_blocks)
    )
    done = lax.fori_loop(0, owners, peel_owner, start)
    per_gain = GB // BB
    for block in range(gain_blocks):
        resid[pl.ds(me_d * group_blocks + block * per_gain, per_gain)] = (
            done[block].reshape(per_gain, BB, columns).astype(BF16)
        )
    resid[block_count] = jnp.zeros((BB, columns), BF16)

    def resid_copy(group, sem, to):
        part = pl.ds(group * group_blocks, group_blocks)
        return pltpu.make_async_remote_copy(
            src_ref=resid.at[part],
            dst_ref=resid.at[part],
            send_sem=r_send.at[sem],
            recv_sem=r_recv.at[group],
            device_id={"dir": to},
            device_id_type=MESH,
        )

    for k in range(1, owners):
        to = lax.rem(me_d + k, owners)
        resid_copy(me_d, to, to).start()
    for k in range(1, owners):
        source = lax.rem(me_d + k, owners)
        resid_copy(source, source, source).wait_recv()

    def rows_copy(src, owner, to):
        return pltpu.make_async_remote_copy(
            src_ref=rows_out.at[src],
            dst_ref=rows_in.at[owner],
            send_sem=d_send.at[src],
            recv_sem=d_recv.at[owner],
            device_id={"tb": to},
            device_id_type=MESH,
        )

    def dispatch(k, carry):
        to = lax.rem(me_t + k, peers)
        for slot in range(slots):
            rows_out[to, slot * BB : (slot + 1) * BB, :] = resid[block_of_ref[to * slots + slot]]

        @pl.when(k < peers)
        def _():
            rows_copy(to, me_t, to).start()

        return carry

    lax.fori_loop(1, peers + 1, dispatch, 0)
    resid_ref[...] = resid[0:block_count].reshape(sample_rows, columns)

    grid_sum = jnp.dot(tables[me_t], rows_out[me_t], preferred_element_type=F32)

    def add_source(k, total):
        source = lax.rem(me_t + k, peers)
        rows_copy(source, source, source).wait_recv()
        return total + jnp.dot(tables[source], rows_in[source], preferred_element_type=F32)

    grid_sum = lax.fori_loop(1, peers, add_source, grid_sum)
    grid_ref[...] = (grid_sum * float(ROWS_DEV) ** (-0.5)).reshape(2, share, columns)

    for k in range(1, owners):
        to = lax.rem(me_d + k, owners)
        resid_copy(me_d, to, to).wait_send()

    def drain(k, carry):
        to = lax.rem(me_t + k, peers)
        rows_copy(to, me_t, to).wait_send()
        return carry

    lax.fori_loop(1, peers, drain, 0)


def local(
    owners,
    peers,
    visibilities,
    uv_coords,
    comp_lm,
    spectra,
    ridge_weight,
    assignment,
    peel_order,
    block_tile,
):
    sample_rows, columns = visibilities.shape
    comps = comp_lm.shape[1]
    block_count = sample_rows // BB
    group_rows = sample_rows // owners
    slots = max(2, 2 * block_count // peers)
    share = PIX // owners

    directions = jnp.arange(DIR_DEV, dtype=jnp.int32)
    place = jnp.sum(
        jnp.where(peel_order[:, None] == directions[None, :], directions[:, None], 0), axis=0
    )
    place = jnp.broadcast_to(place[:, None], (DIR_DEV, comps // DIR_DEV)).reshape(comps)
    entries = jnp.stack([assignment, place])

    tile_ids = block_tile[:, 0]
    block_ids = jnp.arange(block_count, dtype=jnp.int32)
    same_tile = tile_ids[:, None] == tile_ids[None, :]
    before = block_ids[None, :] < block_ids[:, None]
    slot_index = jnp.sum(same_tile & before, axis=1, dtype=jnp.int32)
    target = tile_ids * slots + slot_index
    placed = target[None, :] == jnp.arange(peers * slots, dtype=jnp.int32)[:, None]
    block_of = jnp.min(jnp.where(placed, block_ids[None, :], block_count), axis=1)
    block_coords = uv_coords.reshape(2, block_count, BB).transpose(1, 0, 2).reshape(block_count, -1)
    send_coords = jnp.dot(placed.astype(BF16), block_coords, preferred_element_type=F32)
    send_coords = send_coords.astype(BF16).reshape(peers, slots, 2, BB).transpose(0, 2, 1, 3)
    send_coords = jnp.pad(
        send_coords.reshape(peers, 2, slots * BB), ((0, 0), (0, 14), (0, 0))
    )

    vmem = pl.BlockSpec(memory_space=pltpu.VMEM)
    smem = pl.BlockSpec(memory_space=pltpu.SMEM)
    dma = pltpu.SemaphoreType.DMA
    residual, subgrid = pl.pallas_call(
        functools.partial(kernel, owners, peers, slots),
        out_shape=(
            jax.ShapeDtypeStruct((sample_rows, columns), BF16),
            jax.ShapeDtypeStruct((2, share, columns), F32),
        ),
        in_specs=[vmem] * 6 + [smem, vmem],
        out_specs=(vmem, vmem),
        scratch_shapes=[
            pltpu.VMEM((2, comps, DIR_DEV * columns), BF16),
            pltpu.VMEM((2, group_rows, CHUNK), BF16),
            pltpu.VMEM((2, group_rows, CHUNK), BF16),
            pltpu.VMEM((group_rows, DIR_DEV * columns), F32),
            pltpu.VMEM((owners, group_rows, DIR_DEV * columns), BF16),
            pltpu.VMEM((owners, group_rows, DIR_DEV * columns), BF16),
            pltpu.VMEM((block_count + 1, BB, columns), BF16),
            pltpu.VMEM((peers, slots * BB, columns), BF16),
            pltpu.VMEM((peers, slots * BB, columns), BF16),
            pltpu.VMEM((peers, 16, slots * BB), BF16),
            pltpu.VMEM((peers, 2 * share, slots * BB), BF16),
            dma((owners,)),
            dma((owners,)),
            dma((owners,)),
            dma((owners,)),
            dma((peers,)),
            dma((peers,)),
            dma((peers,)),
            dma((peers,)),
        ],
        compiler_params=pltpu.CompilerParams(
            collective_id=0, has_side_effects=True, vmem_limit_bytes=60 * 1024 * 1024
        ),
    )(
        visibilities,
        uv_coords.astype(F32).T,
        comp_lm,
        spectra,
        ridge_weight[None, :],
        entries,
        block_of,
        send_coords,
    )
    return residual, subgrid[None]


def solution(mesh):
    return jax.shard_map(
        functools.partial(local, mesh.shape["dir"], mesh.shape["tb"]),
        mesh=mesh,
        in_specs=(
            P("tb", None),
            P(None, "tb"),
            P(None, "dir"),
            P(None, "dir", None),
            P(),
            P("dir"),
            P("dir"),
            P("tb", None),
        ),
        out_specs=(P("tb", None), P("tb", None, "dir", None)),
        check_vma=False,
    )
```

```python
import functools
import math

import jax
import jax.numpy as jnp
from jax import lax
from jax.experimental import pallas as pl
from jax.experimental.pallas import tpu as pltpu
from jax.sharding import PartitionSpec as P

NCOMP = 1024
GRID = 32
DIR_DEV = 3
ITERS = 4
BB = 32
GB = 128
ROWS_DEV = 1024
PIX = 1024

MESH = pl.DeviceIdType.MESH
F32 = jnp.float32
BF16 = jnp.bfloat16
LANES = 128
CHUNK = 512
SUB = 32

SIN_FIT = (4.4428795675460835, -7.307816684491791, 3.5977741780872416, -0.7911993921613704)
COS_FIT = (1.414204014809076, -6.977637323456295, 5.715187874756718, -1.728213892223522)


def horner(square, fit):
    total = fit[-1]
    for coefficient in fit[-2::-1]:
        total = total * square + coefficient
    return total


def turn_cos_sin(turns):
    part = turns - jnp.round(turns)
    square = part * part
    half_sin = part * horner(square, SIN_FIT)
    half_cos = horner(square, COS_FIT)
    return (1.0 - half_sin * half_sin).astype(BF16), (half_sin * half_cos).astype(BF16)


def kernel(
    owners,
    peers,
    slots,
    vis_ref,
    uv_ref,
    lm_ref,
    spec_ref,
    ridge_ref,
    entry_ref,
    tile_ref,
    peel_ref,
    resid_ref,
    grid_ref,
    masked,
    lm_parts,
    coord_rows,
    block_row,
    block_of_ref,
    coords_out,
    turned_a,
    turned_b,
    acc,
    models_out,
    models_in,
    resid,
    rows_out,
    rows_in,
    coords_in,
    tables,
    m_send,
    m_recv,
    r_send,
    r_recv,
    d_send,
    d_recv,
    c_send,
    c_recv,
    index_sem,
):
    me_d = lax.axis_index("dir")
    me_t = lax.axis_index("tb")
    sample_rows, columns = vis_ref.shape
    comps = lm_ref.shape[1]
    group_rows = sample_rows // owners
    block_count = sample_rows // BB
    group_blocks = block_count // owners
    slot_rows = slots * BB

    barrier = pltpu.get_barrier_semaphore()
    for k in range(1, owners):
        pl.semaphore_signal(
            barrier, inc=1, device_id={"dir": lax.rem(me_d + k, owners)}, device_id_type=MESH
        )

    def greet(k, carry):
        pl.semaphore_signal(
            barrier, inc=1, device_id={"tb": lax.rem(me_t + k, peers)}, device_id_type=MESH
        )
        return carry

    lax.fori_loop(1, peers, greet, 0)
    pl.semaphore_wait(barrier, owners - 1 + peers - 1)

    slot_lanes = block_row.shape[1]
    lane = lax.broadcasted_iota(jnp.int32, (block_count, slot_lanes), 1)
    tile = jnp.broadcast_to(tile_ref[...], (block_count, slot_lanes))
    named_tile = jnp.where(lane == tile, 1.0, 0.0)
    row_id = lax.broadcasted_iota(jnp.int32, (block_count, block_count), 0)
    earlier = jnp.where(
        lax.broadcasted_iota(jnp.int32, (block_count, block_count), 1) < row_id, 1.0, 0.0
    )
    ranks = jnp.dot(earlier.astype(BF16), named_tile.astype(BF16), preferred_element_type=F32)
    slot = jnp.sum(ranks * named_tile, axis=1, keepdims=True).astype(jnp.int32)
    target = tile_ref[...] * slots + slot
    block_id = lax.broadcasted_iota(jnp.int32, (block_count, slot_lanes), 0)
    taken = jnp.where(lane == target, block_id, block_count).astype(F32)
    block_row[...] = jnp.min(taken, axis=0, keepdims=True).astype(jnp.int32)
    index_copy = pltpu.make_async_copy(block_row, block_of_ref, index_sem)
    index_copy.start()

    u_row = uv_ref[0:1, :].astype(F32)
    v_row = uv_ref[1:2, :].astype(F32)
    stacked = jnp.concatenate(
        [u_row] * 3 + [v_row] * 3 + [jnp.zeros((LANES - 6, sample_rows), F32)], axis=0
    )
    coord_rows[0:block_count] = (
        stacked.T.astype(BF16).reshape(block_count, BB, LANES)
    )
    coord_rows[block_count] = jnp.zeros((BB, LANES), BF16)

    parts = []
    for which in range(2):
        left = lm_ref[which : which + 1, :]
        for part in range(3):
            rounded = left.astype(BF16).astype(F32)
            parts.append(rounded)
            left = left - rounded
    parts.append(jnp.zeros((2, comps), F32))
    lm_parts[...] = jnp.concatenate(parts, axis=0).astype(BF16)

    strips = comps // LANES
    padded = -(-strips // 16) * 16
    named = jnp.concatenate([entry_ref[r : r + 1, :] for r in range(strips)], axis=1)
    places = []
    for direction in range(DIR_DEV):
        value = jnp.int32(0)
        for position in range(DIR_DEV):
            value = value + jnp.where(peel_ref[position] == direction, position, 0)
        places.append(jnp.full((1, comps // DIR_DEV), value, jnp.int32))
    place = jnp.concatenate(places, axis=1).astype(F32)
    low = lax.broadcasted_iota(jnp.int32, (LANES, comps), 0)
    high = lax.broadcasted_iota(jnp.int32, (padded, comps), 0)
    at_low = jnp.where(low == named % LANES, 1.0, 0.0).astype(BF16)
    at_high = jnp.where(high == named // LANES, place, 0.0).astype(BF16)
    positions = lax.dot_general(
        at_low, at_high, (((1,), (1,)), ((), ())), preferred_element_type=F32
    )
    for strip in range(strips):
        own = jnp.broadcast_to(positions[:, strip : strip + 1], (LANES, columns))
        span = pl.ds(strip * LANES, LANES)
        for part in range(2):
            values = spec_ref[part, span, :].astype(F32)
            for position in range(DIR_DEV):
                masked[part, span, position * columns : (position + 1) * columns] = jnp.where(
                    own == float(position), values, 0.0
                ).astype(BF16)

    def coords_copy(src, owner, to):
        return pltpu.make_async_remote_copy(
            src_ref=coords_out.at[src],
            dst_ref=coords_in.at[owner],
            send_sem=c_send.at[src],
            recv_sem=c_recv.at[owner],
            device_id={"tb": to},
            device_id_type=MESH,
        )

    index_copy.wait()

    def block_in(to, slot):
        block = block_of_ref[0, to * slots + slot]
        return jnp.minimum(jnp.maximum(block, 0), block_count)

    def send_coords(k, carry):
        to = lax.rem(me_t + k, peers)
        for slot in range(slots):
            coords_out[to, slot * BB : (slot + 1) * BB, :] = coord_rows[block_in(to, slot)]

        @pl.when(k < peers)
        def _():
            coords_copy(to, me_t, to).start()

        return carry

    lax.fori_loop(1, peers + 1, send_coords, 0)
    coords_in[me_t] = coords_out[me_t]

    def models_copy(group, owner, to):
        return pltpu.make_async_remote_copy(
            src_ref=models_out.at[group],
            dst_ref=models_in.at[owner],
            send_sem=m_send.at[group],
            recv_sem=m_recv.at[owner],
            device_id={"dir": to},
            device_id_type=MESH,
        )

    def predict_group(k, carry):
        group = lax.rem(me_d + k, owners)
        group_coords = coord_rows[pl.ds(group * group_blocks, group_blocks)]
        group_coords = group_coords.reshape(group_rows, LANES)[:, 0:8]
        for chunk in range(comps // CHUNK):
            turned = turned_a if chunk % 2 == 0 else turned_b
            span = slice(chunk * CHUNK, (chunk + 1) * CHUNK)
            turns = jnp.dot(group_coords, lm_parts[:, span], preferred_element_type=F32)
            for sub in range(group_rows // SUB):
                rows = slice(sub * SUB, (sub + 1) * SUB)
                cos_part, sin_part = turn_cos_sin(turns[rows])
                turned[0, rows, :] = cos_part
                turned[1, rows, :] = sin_part
            update = jnp.dot(turned[0], masked[0, span, :], preferred_element_type=F32) + jnp.dot(
                turned[1], masked[1, span, :], preferred_element_type=F32
            )
            if chunk == 0:
                acc[...] = update
            elif chunk < comps // CHUNK - 1:
                acc[...] += update
            else:
                final = (acc[...] + update).astype(BF16)

        @pl.when(k < owners)
        def _():
            models_out[group] = final
            models_copy(group, me_d, group).start()

        @pl.when(k == owners)
        def _():
            models_in[me_d] = final

        return carry

    lax.fori_loop(1, owners + 1, predict_group, 0)

    def wait_coords(k, carry):
        source = lax.rem(me_t + k, peers)
        coords_copy(source, source, source).wait()
        return carry

    lax.fori_loop(1, peers, wait_coords, 0)
    share = grid_ref.shape[1]
    pixel = me_d * share + lax.broadcasted_iota(jnp.int32, (share, LANES), 0)
    which = lax.broadcasted_iota(jnp.int32, (share, LANES), 1)
    pixel_xy = jnp.where(
        which == 0,
        (pixel // GRID - GRID // 2).astype(F32),
        jnp.where(which == 3, (pixel % GRID - GRID // 2).astype(F32), 0.0),
    )
    pixel_xy = (pixel_xy / (2.0 * GRID)).astype(BF16)

    def make_table(source, carry):
        turns = lax.dot_general(
            pixel_xy, coords_in[source], (((1,), (1,)), ((), ())), preferred_element_type=F32
        )
        cos_part, sin_part = turn_cos_sin(turns)
        tables[source, 0:share, :] = cos_part
        tables[source, share : 2 * share, :] = sin_part
        return carry

    lax.fori_loop(0, peers, make_table, 0)

    def wait_models(k, carry):
        source = lax.rem(me_d + k, owners)
        models_copy(source, source, source).wait()
        return carry

    lax.fori_loop(1, owners, wait_models, 0)

    gain_blocks = group_rows // GB
    first = me_d * group_rows
    ridge = jnp.broadcast_to(ridge_ref[...], (8, columns))
    lane = lax.broadcasted_iota(jnp.int32, (8, columns), 1)

    def over_rows(value):
        total = jnp.sum(jnp.sum(value, axis=0), axis=0, keepdims=True)
        return jnp.broadcast_to(total, (8, columns))

    def peel_owner(owner, remains):
        out = []
        for block in range(gain_blocks):
            rest = remains[block]
            for position in range(DIR_DEV):
                model = models_in[
                    owner,
                    block * GB : (block + 1) * GB,
                    position * columns : (position + 1) * columns,
                ].astype(F32)
                model = model.reshape(GB // 8, 8, columns)
                cross_sum = over_rows(rest * model)
                inverse = 1.0 / (over_rows(model * model) + ridge)
                gain = jnp.ones_like(cross_sum)
                for sweep in range(ITERS):
                    before = jnp.where(lane < 2, gain, pltpu.roll(gain, 2, 1))
                    after = jnp.where(
                        lane >= columns - 2, gain, pltpu.roll(gain, columns - 2, 1)
                    )
                    gain = (cross_sum + ridge * (0.5 * (before + after))) * inverse
                rest = rest - gain[None] * model
            out.append(rest.astype(BF16).astype(F32))
        return tuple(out)

    start = tuple(
        vis_ref[pl.ds(pl.multiple_of(first + block * GB, GB), GB), :]
        .astype(F32)
        .reshape(GB // 8, 8, columns)
        for block in range(gain_blocks)
    )
    done = lax.fori_loop(0, owners, peel_owner, start)
    per_gain = GB // BB
    for block in range(gain_blocks):
        resid[pl.ds(me_d * group_blocks + block * per_gain, per_gain)] = (
            done[block].reshape(per_gain, BB, columns).astype(BF16)
        )
    resid[block_count] = jnp.zeros((BB, columns), BF16)

    def resid_copy(group, sem, to):
        part = pl.ds(group * group_blocks, group_blocks)
        return pltpu.make_async_remote_copy(
            src_ref=resid.at[part],
            dst_ref=resid.at[part],
            send_sem=r_send.at[sem],
            recv_sem=r_recv.at[group],
            device_id={"dir": to},
            device_id_type=MESH,
        )

    for k in range(1, owners):
        to = lax.rem(me_d + k, owners)
        resid_copy(me_d, to, to).start()
    for k in range(1, owners):
        source = lax.rem(me_d + k, owners)
        resid_copy(source, source, source).wait_recv()

    def rows_copy(src, owner, to):
        return pltpu.make_async_remote_copy(
            src_ref=rows_out.at[src],
            dst_ref=rows_in.at[owner],
            send_sem=d_send.at[src],
            recv_sem=d_recv.at[owner],
            device_id={"tb": to},
            device_id_type=MESH,
        )

    def dispatch(k, carry):
        to = lax.rem(me_t + k, peers)
        for slot in range(slots):
            rows_out[to, slot * BB : (slot + 1) * BB, :] = resid[block_in(to, slot)]

        @pl.when(k < peers)
        def _():
            rows_copy(to, me_t, to).start()

        return carry

    lax.fori_loop(1, peers + 1, dispatch, 0)
    resid_ref[...] = resid[0:block_count].reshape(sample_rows, columns)

    grid_sum = jnp.dot(tables[me_t], rows_out[me_t], preferred_element_type=F32)

    def add_source(k, total):
        source = lax.rem(me_t + k, peers)
        rows_copy(source, source, source).wait_recv()
        return total + jnp.dot(tables[source], rows_in[source], preferred_element_type=F32)

    grid_sum = lax.fori_loop(1, peers, add_source, grid_sum)
    grid_ref[...] = (grid_sum * float(ROWS_DEV) ** (-0.5)).reshape(2, share, columns)

    for k in range(1, owners):
        to = lax.rem(me_d + k, owners)
        resid_copy(me_d, to, to).wait_send()

    def drain(k, carry):
        to = lax.rem(me_t + k, peers)
        rows_copy(to, me_t, to).wait_send()
        return carry

    lax.fori_loop(1, peers, drain, 0)


def local(
    owners,
    peers,
    visibilities,
    uv_coords,
    comp_lm,
    spectra,
    ridge_weight,
    assignment,
    peel_order,
    block_tile,
):
    sample_rows, columns = visibilities.shape
    comps = comp_lm.shape[1]
    block_count = sample_rows // BB
    slots = max(2, 2 * block_count // peers)
    share = PIX // owners

    slot_lanes = -(-peers * slots // LANES) * LANES
    vmem = pl.BlockSpec(memory_space=pltpu.VMEM)
    smem = pl.BlockSpec(memory_space=pltpu.SMEM)
    dma = pltpu.SemaphoreType.DMA
    residual, subgrid = pl.pallas_call(
        functools.partial(kernel, owners, peers, slots),
        out_shape=(
            jax.ShapeDtypeStruct((sample_rows, columns), BF16),
            jax.ShapeDtypeStruct((2, share, columns), F32),
        ),
        in_specs=[vmem] * 7 + [smem],
        out_specs=(vmem, vmem),
        scratch_shapes=[
            pltpu.VMEM((2, comps, DIR_DEV * columns), BF16),
            pltpu.VMEM((8, comps), BF16),
            pltpu.VMEM((block_count + 1, BB, LANES), BF16),
            pltpu.VMEM((1, slot_lanes), jnp.int32),
            pltpu.SMEM((1, slot_lanes), jnp.int32),
            pltpu.VMEM((peers, slots * BB, LANES), BF16),
            pltpu.VMEM((2, sample_rows // owners, CHUNK), BF16),
            pltpu.VMEM((2, sample_rows // owners, CHUNK), BF16),
            pltpu.VMEM((sample_rows // owners, DIR_DEV * columns), F32),
            pltpu.VMEM((owners, sample_rows // owners, DIR_DEV * columns), BF16),
            pltpu.VMEM((owners, sample_rows // owners, DIR_DEV * columns), BF16),
            pltpu.VMEM((block_count + 1, BB, columns), BF16),
            pltpu.VMEM((peers, slots * BB, columns), BF16),
            pltpu.VMEM((peers, slots * BB, columns), BF16),
            pltpu.VMEM((peers, slots * BB, LANES), BF16),
            pltpu.VMEM((peers, 2 * share, slots * BB), BF16),
            dma((owners,)),
            dma((owners,)),
            dma((owners,)),
            dma((owners,)),
            dma((peers,)),
            dma((peers,)),
            dma((peers,)),
            dma((peers,)),
            dma,
        ],
        compiler_params=pltpu.CompilerParams(
            collective_id=0, has_side_effects=True, vmem_limit_bytes=60 * 1024 * 1024
        ),
    )(
        visibilities,
        uv_coords,
        comp_lm,
        spectra,
        ridge_weight[None, :],
        assignment.reshape(comps // LANES, LANES),
        block_tile,
        peel_order,
    )
    return residual, subgrid[None]


def solution(mesh):
    return jax.shard_map(
        functools.partial(local, mesh.shape["dir"], mesh.shape["tb"]),
        mesh=mesh,
        in_specs=(
            P("tb", None),
            P(None, "tb"),
            P(None, "dir"),
            P(None, "dir", None),
            P(),
            P("dir"),
            P("dir"),
            P("tb", None),
        ),
        out_specs=(P("tb", None), P("tb", None, "dir", None)),
        check_vma=False,
    )
```

```python
import functools
import math

import jax
import jax.numpy as jnp
from jax import lax
from jax.experimental import pallas as pl
from jax.experimental.pallas import tpu as pltpu
from jax.sharding import PartitionSpec as P

NCOMP = 1024
GRID = 32
DIR_DEV = 3
ITERS = 4
BB = 32
GB = 128
ROWS_DEV = 1024
PIX = 1024

MESH = pl.DeviceIdType.MESH
F32 = jnp.float32
BF16 = jnp.bfloat16
LANES = 128
CHUNK = 512
SUB = 32

SIN_FIT = (4.4428795675460835, -7.307816684491791, 3.5977741780872416, -0.7911993921613704)
COS_FIT = (1.414204014809076, -6.977637323456295, 5.715187874756718, -1.728213892223522)


def horner(square, fit):
    total = fit[-1]
    for coefficient in fit[-2::-1]:
        total = total * square + coefficient
    return total


def turn_cos_sin(turns):
    part = turns - jnp.round(turns)
    square = part * part
    half_sin = part * horner(square, SIN_FIT)
    half_cos = horner(square, COS_FIT)
    return (1.0 - half_sin * half_sin).astype(BF16), (half_sin * half_cos).astype(BF16)


def kernel(
    owners,
    peers,
    slots,
    vis_ref,
    uv_ref,
    lm_ref,
    spec_ref,
    ridge_ref,
    entry_ref,
    tile_ref,
    peel_ref,
    resid_ref,
    grid_ref,
    masked,
    lm_parts,
    coord_rows,
    block_row,
    block_of_ref,
    coords_out,
    turned_a,
    turned_b,
    acc,
    models_out,
    models_in,
    resid,
    rows_out,
    rows_in,
    coords_in,
    tables,
    m_send,
    m_recv,
    r_send,
    r_recv,
    d_send,
    d_recv,
    c_send,
    c_recv,
    index_sem,
):
    me_d = lax.axis_index("dir")
    me_t = lax.axis_index("tb")
    sample_rows, columns = vis_ref.shape
    comps = lm_ref.shape[1]
    group_rows = sample_rows // owners
    block_count = sample_rows // BB
    group_blocks = block_count // owners
    slot_rows = slots * BB

    barrier = pltpu.get_barrier_semaphore()
    for k in range(1, owners):
        pl.semaphore_signal(
            barrier, inc=1, device_id={"dir": lax.rem(me_d + k, owners)}, device_id_type=MESH
        )

    def greet(k, carry):
        pl.semaphore_signal(
            barrier, inc=1, device_id={"tb": lax.rem(me_t + k, peers)}, device_id_type=MESH
        )
        return carry

    lax.fori_loop(1, peers, greet, 0)
    pl.semaphore_wait(barrier, owners - 1 + peers - 1)

    slot_lanes = block_row.shape[1]
    tiles = jnp.broadcast_to(tile_ref[...], (slot_lanes, block_count))
    named_tile = jnp.where(
        lax.broadcasted_iota(jnp.int32, (slot_lanes, block_count), 0) == tiles, 1.0, 0.0
    )
    earlier = jnp.where(
        lax.broadcasted_iota(jnp.int32, (block_count, block_count), 0)
        < lax.broadcasted_iota(jnp.int32, (block_count, block_count), 1),
        1.0,
        0.0,
    )
    ranks = jnp.dot(named_tile.astype(BF16), earlier.astype(BF16), preferred_element_type=F32)
    slot = jnp.sum(ranks * named_tile, axis=0, keepdims=True).astype(jnp.int32)
    target = jnp.broadcast_to(tile_ref[...] * slots + slot, (slot_lanes, block_count))
    lane = lax.broadcasted_iota(jnp.int32, (slot_lanes, block_count), 0)
    taken = jnp.where(lane == target, 1.0, 0.0).astype(BF16)
    block_id = lax.broadcasted_iota(jnp.int32, (8, block_count), 1) - block_count
    picked = lax.dot_general(
        block_id.astype(F32).astype(BF16),
        taken,
        (((1,), (1,)), ((), ())),
        preferred_element_type=F32,
    )
    block_row[...] = picked[0:1, :].astype(jnp.int32) + block_count
    index_copy = pltpu.make_async_copy(block_row, block_of_ref, index_sem)
    index_copy.start()

    u_row = uv_ref[0:1, :].astype(F32)
    v_row = uv_ref[1:2, :].astype(F32)
    stacked = jnp.concatenate(
        [u_row] * 3 + [v_row] * 3 + [jnp.zeros((LANES - 6, sample_rows), F32)], axis=0
    )
    coord_rows[0:block_count] = (
        stacked.T.astype(BF16).reshape(block_count, BB, LANES)
    )
    coord_rows[block_count] = jnp.zeros((BB, LANES), BF16)

    parts = []
    for which in range(2):
        left = lm_ref[which : which + 1, :]
        for part in range(3):
            rounded = left.astype(BF16).astype(F32)
            parts.append(rounded)
            left = left - rounded
    parts.append(jnp.zeros((2, comps), F32))
    lm_parts[...] = jnp.concatenate(parts, axis=0).astype(BF16)

    strips = comps // LANES
    padded = -(-strips // 16) * 16
    named = jnp.concatenate([entry_ref[r : r + 1, :] for r in range(strips)], axis=1)
    places = []
    for direction in range(DIR_DEV):
        value = jnp.int32(0)
        for position in range(DIR_DEV):
            value = value + jnp.where(peel_ref[position] == direction, position, 0)
        places.append(jnp.full((1, comps // DIR_DEV), value, jnp.int32))
    place = jnp.concatenate(places, axis=1).astype(F32)
    low = lax.broadcasted_iota(jnp.int32, (LANES, comps), 0)
    high = lax.broadcasted_iota(jnp.int32, (padded, comps), 0)
    at_low = jnp.where(low == named % LANES, 1.0, 0.0).astype(BF16)
    at_high = jnp.where(high == named // LANES, place, 0.0).astype(BF16)
    positions = lax.dot_general(
        at_low, at_high, (((1,), (1,)), ((), ())), preferred_element_type=F32
    )
    for strip in range(strips):
        own = jnp.broadcast_to(positions[:, strip : strip + 1], (LANES, columns))
        span = pl.ds(strip * LANES, LANES)
        for part in range(2):
            values = spec_ref[part, span, :].astype(F32)
            for position in range(DIR_DEV):
                masked[part, span, position * columns : (position + 1) * columns] = jnp.where(
                    own == float(position), values, 0.0
                ).astype(BF16)

    def coords_copy(src, owner, to):
        return pltpu.make_async_remote_copy(
            src_ref=coords_out.at[src],
            dst_ref=coords_in.at[owner],
            send_sem=c_send.at[src],
            recv_sem=c_recv.at[owner],
            device_id={"tb": to},
            device_id_type=MESH,
        )

    index_copy.wait()

    def block_in(to, slot):
        block = block_of_ref[0, to * slots + slot]
        return jnp.minimum(jnp.maximum(block, 0), block_count)

    def send_coords(k, carry):
        to = lax.rem(me_t + k, peers)
        for slot in range(slots):
            coords_out[to, slot * BB : (slot + 1) * BB, :] = coord_rows[block_in(to, slot)]

        @pl.when(k < peers)
        def _():
            coords_copy(to, me_t, to).start()

        return carry

    lax.fori_loop(1, peers + 1, send_coords, 0)
    coords_in[me_t] = coords_out[me_t]

    def models_copy(group, owner, to):
        return pltpu.make_async_remote_copy(
            src_ref=models_out.at[group],
            dst_ref=models_in.at[owner],
            send_sem=m_send.at[group],
            recv_sem=m_recv.at[owner],
            device_id={"dir": to},
            device_id_type=MESH,
        )

    def predict_group(k, carry):
        group = lax.rem(me_d + k, owners)
        group_coords = coord_rows[pl.ds(group * group_blocks, group_blocks)]
        group_coords = group_coords.reshape(group_rows, LANES)[:, 0:8]
        chunks = comps // CHUNK
        buffers = (turned_a, turned_b)
        pieces = group_rows // SUB

        def spread_turns(chunk):
            return jnp.dot(
                group_coords,
                lm_parts[:, chunk * CHUNK : (chunk + 1) * CHUNK],
                preferred_element_type=F32,
            )

        def contract_chunk(chunk, part):
            return jnp.dot(
                buffers[chunk % 2][part],
                masked[part, chunk * CHUNK : (chunk + 1) * CHUNK, :],
                preferred_element_type=F32,
            )

        turns = spread_turns(0)
        for chunk in range(chunks):
            turned = buffers[chunk % 2]
            following = None
            for sub in range(pieces):
                rows = slice(sub * SUB, (sub + 1) * SUB)
                cos_part, sin_part = turn_cos_sin(turns[rows])
                turned[0, rows, :] = cos_part
                turned[1, rows, :] = sin_part
                if chunk > 0 and sub == 0:
                    update = contract_chunk(chunk - 1, 0)
                if chunk > 0 and sub == pieces // 2 - 1:
                    update = update + contract_chunk(chunk - 1, 1)
                    if chunk == 1:
                        acc[...] = update
                    else:
                        acc[...] += update
                if chunk + 1 < chunks and sub == pieces - 2:
                    following = spread_turns(chunk + 1)
            turns = following
        last = contract_chunk(chunks - 1, 0) + contract_chunk(chunks - 1, 1)
        final = (acc[...] + last).astype(BF16)

        @pl.when(k < owners)
        def _():
            models_out[group] = final
            models_copy(group, me_d, group).start()

        @pl.when(k == owners)
        def _():
            models_in[me_d] = final

        return carry

    lax.fori_loop(1, owners + 1, predict_group, 0)

    def wait_coords(k, carry):
        source = lax.rem(me_t + k, peers)
        coords_copy(source, source, source).wait()
        return carry

    lax.fori_loop(1, peers, wait_coords, 0)
    share = grid_ref.shape[1]
    pixel = me_d * share + lax.broadcasted_iota(jnp.int32, (share, LANES), 0)
    which = lax.broadcasted_iota(jnp.int32, (share, LANES), 1)
    pixel_xy = jnp.where(
        which == 0,
        (pixel // GRID - GRID // 2).astype(F32),
        jnp.where(which == 3, (pixel % GRID - GRID // 2).astype(F32), 0.0),
    )
    pixel_xy = (pixel_xy / (2.0 * GRID)).astype(BF16)

    def make_table(source, carry):
        turns = lax.dot_general(
            pixel_xy, coords_in[source], (((1,), (1,)), ((), ())), preferred_element_type=F32
        )
        cos_part, sin_part = turn_cos_sin(turns)
        tables[source, 0:share, :] = cos_part
        tables[source, share : 2 * share, :] = sin_part
        return carry

    lax.fori_loop(0, peers, make_table, 0)

    def wait_models(k, carry):
        source = lax.rem(me_d + k, owners)
        models_copy(source, source, source).wait()
        return carry

    lax.fori_loop(1, owners, wait_models, 0)

    gain_blocks = group_rows // GB
    first = me_d * group_rows
    ridge = jnp.broadcast_to(ridge_ref[...], (8, columns))
    lane = lax.broadcasted_iota(jnp.int32, (8, columns), 1)

    def over_rows(value):
        total = jnp.sum(jnp.sum(value, axis=0), axis=0, keepdims=True)
        return jnp.broadcast_to(total, (8, columns))

    def peel_owner(owner, remains):
        out = []
        for block in range(gain_blocks):
            rest = remains[block]
            for position in range(DIR_DEV):
                model = models_in[
                    owner,
                    block * GB : (block + 1) * GB,
                    position * columns : (position + 1) * columns,
                ].astype(F32)
                model = model.reshape(GB // 8, 8, columns)
                cross_sum = over_rows(rest * model)
                inverse = 1.0 / (over_rows(model * model) + ridge)
                gain = jnp.ones_like(cross_sum)
                for sweep in range(ITERS):
                    before = jnp.where(lane < 2, gain, pltpu.roll(gain, 2, 1))
                    after = jnp.where(
                        lane >= columns - 2, gain, pltpu.roll(gain, columns - 2, 1)
                    )
                    gain = (cross_sum + ridge * (0.5 * (before + after))) * inverse
                rest = rest - gain[None] * model
            out.append(rest.astype(BF16).astype(F32))
        return tuple(out)

    start = tuple(
        vis_ref[pl.ds(pl.multiple_of(first + block * GB, GB), GB), :]
        .astype(F32)
        .reshape(GB // 8, 8, columns)
        for block in range(gain_blocks)
    )
    done = lax.fori_loop(0, owners, peel_owner, start)
    per_gain = GB // BB
    for block in range(gain_blocks):
        resid[pl.ds(me_d * group_blocks + block * per_gain, per_gain)] = (
            done[block].reshape(per_gain, BB, columns).astype(BF16)
        )
    resid[block_count] = jnp.zeros((BB, columns), BF16)

    def resid_copy(group, sem, to):
        part = pl.ds(group * group_blocks, group_blocks)
        return pltpu.make_async_remote_copy(
            src_ref=resid.at[part],
            dst_ref=resid.at[part],
            send_sem=r_send.at[sem],
            recv_sem=r_recv.at[group],
            device_id={"dir": to},
            device_id_type=MESH,
        )

    for k in range(1, owners):
        to = lax.rem(me_d + k, owners)
        resid_copy(me_d, to, to).start()
    for k in range(1, owners):
        source = lax.rem(me_d + k, owners)
        resid_copy(source, source, source).wait_recv()

    def rows_copy(src, owner, to):
        return pltpu.make_async_remote_copy(
            src_ref=rows_out.at[src],
            dst_ref=rows_in.at[owner],
            send_sem=d_send.at[src],
            recv_sem=d_recv.at[owner],
            device_id={"tb": to},
            device_id_type=MESH,
        )

    def dispatch(k, carry):
        to = lax.rem(me_t + k, peers)
        for slot in range(slots):
            rows_out[to, slot * BB : (slot + 1) * BB, :] = resid[block_in(to, slot)]

        @pl.when(k < peers)
        def _():
            rows_copy(to, me_t, to).start()

        return carry

    lax.fori_loop(1, peers + 1, dispatch, 0)
    resid_ref[...] = resid[0:block_count].reshape(sample_rows, columns)

    grid_sum = jnp.dot(tables[me_t], rows_out[me_t], preferred_element_type=F32)

    def add_source(k, total):
        source = lax.rem(me_t + k, peers)
        rows_copy(source, source, source).wait_recv()
        return total + jnp.dot(tables[source], rows_in[source], preferred_element_type=F32)

    grid_sum = lax.fori_loop(1, peers, add_source, grid_sum)
    grid_ref[...] = (grid_sum * float(ROWS_DEV) ** (-0.5)).reshape(2, share, columns)

    for k in range(1, owners):
        to = lax.rem(me_d + k, owners)
        resid_copy(me_d, to, to).wait_send()

    def drain(k, carry):
        to = lax.rem(me_t + k, peers)
        rows_copy(to, me_t, to).wait_send()
        return carry

    lax.fori_loop(1, peers, drain, 0)


def local(
    owners,
    peers,
    visibilities,
    uv_coords,
    comp_lm,
    spectra,
    ridge_weight,
    assignment,
    peel_order,
    block_tile,
):
    sample_rows, columns = visibilities.shape
    comps = comp_lm.shape[1]
    block_count = sample_rows // BB
    slots = max(2, 2 * block_count // peers)
    share = PIX // owners

    slot_lanes = -(-peers * slots // LANES) * LANES
    vmem = pl.BlockSpec(memory_space=pltpu.VMEM)
    smem = pl.BlockSpec(memory_space=pltpu.SMEM)
    dma = pltpu.SemaphoreType.DMA
    residual, subgrid = pl.pallas_call(
        functools.partial(kernel, owners, peers, slots),
        out_shape=(
            jax.ShapeDtypeStruct((sample_rows, columns), BF16),
            jax.ShapeDtypeStruct((2, share, columns), F32),
        ),
        in_specs=[vmem] * 7 + [smem],
        out_specs=(vmem, vmem),
        scratch_shapes=[
            pltpu.VMEM((2, comps, DIR_DEV * columns), BF16),
            pltpu.VMEM((8, comps), BF16),
            pltpu.VMEM((block_count + 1, BB, LANES), BF16),
            pltpu.VMEM((1, slot_lanes), jnp.int32),
            pltpu.SMEM((1, slot_lanes), jnp.int32),
            pltpu.VMEM((peers, slots * BB, LANES), BF16),
            pltpu.VMEM((2, sample_rows // owners, CHUNK), BF16),
            pltpu.VMEM((2, sample_rows // owners, CHUNK), BF16),
            pltpu.VMEM((sample_rows // owners, DIR_DEV * columns), F32),
            pltpu.VMEM((owners, sample_rows // owners, DIR_DEV * columns), BF16),
            pltpu.VMEM((owners, sample_rows // owners, DIR_DEV * columns), BF16),
            pltpu.VMEM((block_count + 1, BB, columns), BF16),
            pltpu.VMEM((peers, slots * BB, columns), BF16),
            pltpu.VMEM((peers, slots * BB, columns), BF16),
            pltpu.VMEM((peers, slots * BB, LANES), BF16),
            pltpu.VMEM((peers, 2 * share, slots * BB), BF16),
            dma((owners,)),
            dma((owners,)),
            dma((owners,)),
            dma((owners,)),
            dma((peers,)),
            dma((peers,)),
            dma((peers,)),
            dma((peers,)),
            dma,
        ],
        compiler_params=pltpu.CompilerParams(
            collective_id=0, has_side_effects=True, vmem_limit_bytes=60 * 1024 * 1024
        ),
    )(
        visibilities,
        uv_coords,
        comp_lm,
        spectra,
        ridge_weight[None, :],
        assignment.reshape(comps // LANES, LANES),
        block_tile.reshape(1, block_count),
        peel_order,
    )
    return residual, subgrid[None]


def solution(mesh):
    return jax.shard_map(
        functools.partial(local, mesh.shape["dir"], mesh.shape["tb"]),
        mesh=mesh,
        in_specs=(
            P("tb", None),
            P(None, "tb"),
            P(None, "dir"),
            P(None, "dir", None),
            P(),
            P("dir"),
            P("dir"),
            P("tb", None),
        ),
        out_specs=(P("tb", None), P("tb", None, "dir", None)),
        check_vma=False,
    )
```

```python
import functools
import math

import jax
import jax.numpy as jnp
from jax import lax
from jax.experimental import pallas as pl
from jax.experimental.pallas import tpu as pltpu
from jax.sharding import PartitionSpec as P

NCOMP = 1024
GRID = 32
DIR_DEV = 3
ITERS = 4
BB = 32
GB = 128
ROWS_DEV = 1024
PIX = 1024

MESH = pl.DeviceIdType.MESH
F32 = jnp.float32
BF16 = jnp.bfloat16
LANES = 128
CHUNK = 256
SUB = 32

SIN_FIT = (4.4428795675460835, -7.307816684491791, 3.5977741780872416, -0.7911993921613704)
COS_FIT = (1.414204014809076, -6.977637323456295, 5.715187874756718, -1.728213892223522)


def horner(square, fit):
    total = fit[-1]
    for coefficient in fit[-2::-1]:
        total = total * square + coefficient
    return total


def turn_cos_sin(turns):
    part = turns - jnp.round(turns)
    square = part * part
    half_sin = part * horner(square, SIN_FIT)
    half_cos = horner(square, COS_FIT)
    return (1.0 - half_sin * half_sin).astype(BF16), (half_sin * half_cos).astype(BF16)


def kernel(
    owners,
    peers,
    slots,
    vis_ref,
    uv_ref,
    lm_ref,
    spec_ref,
    ridge_ref,
    entry_ref,
    tile_ref,
    peel_ref,
    resid_ref,
    grid_ref,
    masked,
    lm_parts,
    coord_rows,
    block_row,
    block_of_ref,
    coords_out,
    turned_a,
    turned_b,
    acc,
    models_out,
    models_in,
    resid,
    rows_out,
    rows_in,
    coords_in,
    tables,
    m_send,
    m_recv,
    r_send,
    r_recv,
    d_send,
    d_recv,
    c_send,
    c_recv,
    index_sem,
):
    me_d = lax.axis_index("dir")
    me_t = lax.axis_index("tb")
    sample_rows, columns = vis_ref.shape
    comps = lm_ref.shape[1]
    group_rows = sample_rows // owners
    block_count = sample_rows // BB
    group_blocks = block_count // owners
    slot_rows = slots * BB

    barrier = pltpu.get_barrier_semaphore()
    for k in range(1, owners):
        pl.semaphore_signal(
            barrier, inc=1, device_id={"dir": lax.rem(me_d + k, owners)}, device_id_type=MESH
        )

    def greet(k, carry):
        pl.semaphore_signal(
            barrier, inc=1, device_id={"tb": lax.rem(me_t + k, peers)}, device_id_type=MESH
        )
        return carry

    lax.fori_loop(1, peers, greet, 0)
    pl.semaphore_wait(barrier, owners - 1 + peers - 1)

    slot_lanes = block_row.shape[1]
    tiles = jnp.broadcast_to(tile_ref[...], (slot_lanes, block_count))
    named_tile = jnp.where(
        lax.broadcasted_iota(jnp.int32, (slot_lanes, block_count), 0) == tiles, 1.0, 0.0
    )
    earlier = jnp.where(
        lax.broadcasted_iota(jnp.int32, (block_count, block_count), 0)
        < lax.broadcasted_iota(jnp.int32, (block_count, block_count), 1),
        1.0,
        0.0,
    )
    ranks = jnp.dot(named_tile.astype(BF16), earlier.astype(BF16), preferred_element_type=F32)
    slot = jnp.sum(ranks * named_tile, axis=0, keepdims=True).astype(jnp.int32)
    target = jnp.broadcast_to(tile_ref[...] * slots + slot, (slot_lanes, block_count))
    lane = lax.broadcasted_iota(jnp.int32, (slot_lanes, block_count), 0)
    taken = jnp.where(lane == target, 1.0, 0.0).astype(BF16)
    block_id = lax.broadcasted_iota(jnp.int32, (8, block_count), 1) - block_count
    picked = lax.dot_general(
        block_id.astype(F32).astype(BF16),
        taken,
        (((1,), (1,)), ((), ())),
        preferred_element_type=F32,
    )
    block_row[...] = picked[0:1, :].astype(jnp.int32) + block_count
    index_copy = pltpu.make_async_copy(block_row, block_of_ref, index_sem)
    index_copy.start()

    u_row = uv_ref[0:1, :].astype(F32)
    v_row = uv_ref[1:2, :].astype(F32)
    stacked = jnp.concatenate(
        [u_row] * 3 + [v_row] * 3 + [jnp.zeros((LANES - 6, sample_rows), F32)], axis=0
    )
    coord_rows[0:block_count] = (
        stacked.T.astype(BF16).reshape(block_count, BB, LANES)
    )
    coord_rows[block_count] = jnp.zeros((BB, LANES), BF16)

    parts = []
    for which in range(2):
        left = lm_ref[which : which + 1, :]
        for part in range(3):
            rounded = left.astype(BF16).astype(F32)
            parts.append(rounded)
            left = left - rounded
    parts.append(jnp.zeros((2, comps), F32))
    lm_parts[...] = jnp.concatenate(parts, axis=0).astype(BF16)

    strips = comps // LANES
    padded = -(-strips // 16) * 16
    named = jnp.concatenate([entry_ref[r : r + 1, :] for r in range(strips)], axis=1)
    places = []
    for direction in range(DIR_DEV):
        value = jnp.int32(0)
        for position in range(DIR_DEV):
            value = value + jnp.where(peel_ref[position] == direction, position, 0)
        places.append(jnp.full((1, comps // DIR_DEV), value, jnp.int32))
    place = jnp.concatenate(places, axis=1).astype(F32)
    low = lax.broadcasted_iota(jnp.int32, (LANES, comps), 0)
    high = lax.broadcasted_iota(jnp.int32, (padded, comps), 0)
    at_low = jnp.where(low == named % LANES, 1.0, 0.0).astype(BF16)
    at_high = jnp.where(high == named // LANES, place, 0.0).astype(BF16)
    positions = lax.dot_general(
        at_low, at_high, (((1,), (1,)), ((), ())), preferred_element_type=F32
    )
    for strip in range(strips):
        own = jnp.broadcast_to(positions[:, strip : strip + 1], (LANES, columns)).astype(BF16)
        span = pl.ds(strip * LANES, LANES)
        for part in range(2):
            values = spec_ref[part, span, :]
            for position in range(DIR_DEV):
                masked[part, span, position * columns : (position + 1) * columns] = jnp.where(
                    own == jnp.asarray(position, BF16), values, jnp.zeros_like(values)
                )

    def coords_copy(src, owner, to):
        return pltpu.make_async_remote_copy(
            src_ref=coords_out.at[src],
            dst_ref=coords_in.at[owner],
            send_sem=c_send.at[src],
            recv_sem=c_recv.at[owner],
            device_id={"tb": to},
            device_id_type=MESH,
        )

    index_copy.wait()

    def block_in(to, slot):
        block = block_of_ref[0, to * slots + slot]
        return jnp.minimum(jnp.maximum(block, 0), block_count)

    def send_coords(k, carry):
        to = lax.rem(me_t + k, peers)
        for slot in range(slots):
            coords_out[to, slot * BB : (slot + 1) * BB, :] = coord_rows[block_in(to, slot)]

        @pl.when(k < peers)
        def _():
            coords_copy(to, me_t, to).start()

        return carry

    lax.fori_loop(1, peers + 1, send_coords, 0)
    coords_in[me_t] = coords_out[me_t]

    def models_copy(group, owner, to):
        return pltpu.make_async_remote_copy(
            src_ref=models_out.at[group],
            dst_ref=models_in.at[owner],
            send_sem=m_send.at[group],
            recv_sem=m_recv.at[owner],
            device_id={"dir": to},
            device_id_type=MESH,
        )

    def predict_group(k, carry):
        group = lax.rem(me_d + k, owners)
        group_coords = coord_rows[pl.ds(group * group_blocks, group_blocks)]
        group_coords = group_coords.reshape(group_rows, LANES)[:, 0:8]
        chunks = comps // CHUNK
        buffers = (turned_a, turned_b)
        pieces = group_rows // SUB

        def spread_turns(chunk):
            return jnp.dot(
                group_coords,
                lm_parts[:, chunk * CHUNK : (chunk + 1) * CHUNK],
                preferred_element_type=F32,
            )

        def contract_chunk(chunk, part):
            return jnp.dot(
                buffers[chunk % 2][part],
                masked[part, chunk * CHUNK : (chunk + 1) * CHUNK, :],
                preferred_element_type=F32,
            )

        turns = spread_turns(0)
        for chunk in range(chunks):
            turned = buffers[chunk % 2]
            following = None
            for sub in range(pieces):
                rows = slice(sub * SUB, (sub + 1) * SUB)
                cos_part, sin_part = turn_cos_sin(turns[rows])
                turned[0, rows, :] = cos_part
                turned[1, rows, :] = sin_part
                if chunk > 0 and sub == 0:
                    update = contract_chunk(chunk - 1, 0)
                if chunk > 0 and sub == pieces // 2 - 1:
                    update = update + contract_chunk(chunk - 1, 1)
                    if chunk == 1:
                        acc[...] = update
                    else:
                        acc[...] += update
                if chunk + 1 < chunks and sub == pieces - 2:
                    following = spread_turns(chunk + 1)
            turns = following
        last = contract_chunk(chunks - 1, 0) + contract_chunk(chunks - 1, 1)
        final = (acc[...] + last).astype(BF16)

        @pl.when(k < owners)
        def _():
            models_out[group] = final
            models_copy(group, me_d, group).start()

        @pl.when(k == owners)
        def _():
            models_in[me_d] = final

        return carry

    lax.fori_loop(1, owners + 1, predict_group, 0)

    def wait_coords(k, carry):
        source = lax.rem(me_t + k, peers)
        coords_copy(source, source, source).wait()
        return carry

    lax.fori_loop(1, peers, wait_coords, 0)
    share = grid_ref.shape[1]
    pixel = me_d * share + lax.broadcasted_iota(jnp.int32, (share, LANES), 0)
    which = lax.broadcasted_iota(jnp.int32, (share, LANES), 1)
    pixel_xy = jnp.where(
        which == 0,
        (pixel // GRID - GRID // 2).astype(F32),
        jnp.where(which == 3, (pixel % GRID - GRID // 2).astype(F32), 0.0),
    )
    pixel_xy = (pixel_xy / (2.0 * GRID)).astype(BF16)

    def make_table(source, carry):
        turns = lax.dot_general(
            pixel_xy, coords_in[source], (((1,), (1,)), ((), ())), preferred_element_type=F32
        )
        cos_part, sin_part = turn_cos_sin(turns)
        tables[source, 0:share, :] = cos_part
        tables[source, share : 2 * share, :] = sin_part
        return carry

    lax.fori_loop(0, peers, make_table, 0)

    def wait_models(k, carry):
        source = lax.rem(me_d + k, owners)
        models_copy(source, source, source).wait()
        return carry

    lax.fori_loop(1, owners, wait_models, 0)

    gain_blocks = group_rows // GB
    first = me_d * group_rows
    ridge = jnp.broadcast_to(ridge_ref[...], (8, columns))
    lane = lax.broadcasted_iota(jnp.int32, (8, columns), 1)

    def over_rows(value):
        total = jnp.sum(jnp.sum(value, axis=0), axis=0, keepdims=True)
        return jnp.broadcast_to(total, (8, columns))

    def peel_owner(owner, remains):
        out = []
        for block in range(gain_blocks):
            rest = remains[block]
            for position in range(DIR_DEV):
                model = models_in[
                    owner,
                    block * GB : (block + 1) * GB,
                    position * columns : (position + 1) * columns,
                ].astype(F32)
                model = model.reshape(GB // 8, 8, columns)
                cross_sum = over_rows(rest * model)
                inverse = 1.0 / (over_rows(model * model) + ridge)
                gain = jnp.ones_like(cross_sum)
                for sweep in range(ITERS):
                    before = jnp.where(lane < 2, gain, pltpu.roll(gain, 2, 1))
                    after = jnp.where(
                        lane >= columns - 2, gain, pltpu.roll(gain, columns - 2, 1)
                    )
                    gain = (cross_sum + ridge * (0.5 * (before + after))) * inverse
                rest = rest - gain[None] * model
            out.append(rest.astype(BF16).astype(F32))
        return tuple(out)

    start = tuple(
        vis_ref[pl.ds(pl.multiple_of(first + block * GB, GB), GB), :]
        .astype(F32)
        .reshape(GB // 8, 8, columns)
        for block in range(gain_blocks)
    )
    done = lax.fori_loop(0, owners, peel_owner, start)
    per_gain = GB // BB
    for block in range(gain_blocks):
        resid[pl.ds(me_d * group_blocks + block * per_gain, per_gain)] = (
            done[block].reshape(per_gain, BB, columns).astype(BF16)
        )
    resid[block_count] = jnp.zeros((BB, columns), BF16)

    def resid_copy(group, sem, to):
        part = pl.ds(group * group_blocks, group_blocks)
        return pltpu.make_async_remote_copy(
            src_ref=resid.at[part],
            dst_ref=resid.at[part],
            send_sem=r_send.at[sem],
            recv_sem=r_recv.at[group],
            device_id={"dir": to},
            device_id_type=MESH,
        )

    for k in range(1, owners):
        to = lax.rem(me_d + k, owners)
        resid_copy(me_d, to, to).start()
    for k in range(1, owners):
        source = lax.rem(me_d + k, owners)
        resid_copy(source, source, source).wait_recv()

    def rows_copy(src, owner, to):
        return pltpu.make_async_remote_copy(
            src_ref=rows_out.at[src],
            dst_ref=rows_in.at[owner],
            send_sem=d_send.at[src],
            recv_sem=d_recv.at[owner],
            device_id={"tb": to},
            device_id_type=MESH,
        )

    def dispatch(k, carry):
        to = lax.rem(me_t + k, peers)
        for slot in range(slots):
            rows_out[to, slot * BB : (slot + 1) * BB, :] = resid[block_in(to, slot)]

        @pl.when(k < peers)
        def _():
            rows_copy(to, me_t, to).start()

        return carry

    lax.fori_loop(1, peers + 1, dispatch, 0)
    resid_ref[...] = resid[0:block_count].reshape(sample_rows, columns)

    grid_sum = jnp.dot(tables[me_t], rows_out[me_t], preferred_element_type=F32)

    def add_source(k, total):
        source = lax.rem(me_t + k, peers)
        rows_copy(source, source, source).wait_recv()
        return total + jnp.dot(tables[source], rows_in[source], preferred_element_type=F32)

    grid_sum = lax.fori_loop(1, peers, add_source, grid_sum)
    grid_ref[...] = (grid_sum * float(ROWS_DEV) ** (-0.5)).reshape(2, share, columns)

    for k in range(1, owners):
        to = lax.rem(me_d + k, owners)
        resid_copy(me_d, to, to).wait_send()

    def drain(k, carry):
        to = lax.rem(me_t + k, peers)
        rows_copy(to, me_t, to).wait_send()
        return carry

    lax.fori_loop(1, peers, drain, 0)


def finish(resid_ref, grid_ref, resid_out, grid_out, sem):
    copies = (
        pltpu.make_async_copy(resid_ref, resid_out, sem.at[0]),
        pltpu.make_async_copy(grid_ref, grid_out, sem.at[1]),
    )
    for copy in copies:
        copy.start()
    for copy in copies:
        copy.wait()


def local(
    owners,
    peers,
    visibilities,
    uv_coords,
    comp_lm,
    spectra,
    ridge_weight,
    assignment,
    peel_order,
    block_tile,
):
    sample_rows, columns = visibilities.shape
    comps = comp_lm.shape[1]
    block_count = sample_rows // BB
    slots = max(2, 2 * block_count // peers)
    share = PIX // owners

    slot_lanes = -(-peers * slots // LANES) * LANES
    vmem = pl.BlockSpec(memory_space=pltpu.VMEM)
    smem = pl.BlockSpec(memory_space=pltpu.SMEM)
    dma = pltpu.SemaphoreType.DMA
    residual, subgrid = pl.pallas_call(
        functools.partial(kernel, owners, peers, slots),
        out_shape=(
            jax.ShapeDtypeStruct((sample_rows, columns), BF16),
            jax.ShapeDtypeStruct((2, share, columns), F32),
        ),
        in_specs=[vmem] * 7 + [smem],
        out_specs=(vmem, vmem),
        scratch_shapes=[
            pltpu.VMEM((2, comps, DIR_DEV * columns), BF16),
            pltpu.VMEM((8, comps), BF16),
            pltpu.VMEM((block_count + 1, BB, LANES), BF16),
            pltpu.VMEM((1, slot_lanes), jnp.int32),
            pltpu.SMEM((1, slot_lanes), jnp.int32),
            pltpu.VMEM((peers, slots * BB, LANES), BF16),
            pltpu.VMEM((2, sample_rows // owners, CHUNK), BF16),
            pltpu.VMEM((2, sample_rows // owners, CHUNK), BF16),
            pltpu.VMEM((sample_rows // owners, DIR_DEV * columns), F32),
            pltpu.VMEM((owners, sample_rows // owners, DIR_DEV * columns), BF16),
            pltpu.VMEM((owners, sample_rows // owners, DIR_DEV * columns), BF16),
            pltpu.VMEM((block_count + 1, BB, columns), BF16),
            pltpu.VMEM((peers, slots * BB, columns), BF16),
            pltpu.VMEM((peers, slots * BB, columns), BF16),
            pltpu.VMEM((peers, slots * BB, LANES), BF16),
            pltpu.VMEM((peers, 2 * share, slots * BB), BF16),
            dma((owners,)),
            dma((owners,)),
            dma((owners,)),
            dma((owners,)),
            dma((peers,)),
            dma((peers,)),
            dma((peers,)),
            dma((peers,)),
            dma,
        ],
        compiler_params=pltpu.CompilerParams(
            collective_id=0, has_side_effects=True, vmem_limit_bytes=60 * 1024 * 1024
        ),
    )(
        visibilities,
        uv_coords,
        comp_lm,
        spectra,
        ridge_weight[None, :],
        assignment.reshape(comps // LANES, LANES),
        block_tile.reshape(1, block_count),
        peel_order,
    )
    anywhere = pl.BlockSpec(memory_space=pl.ANY)
    residual, subgrid = pl.pallas_call(
        finish,
        out_shape=(
            jax.ShapeDtypeStruct(residual.shape, residual.dtype),
            jax.ShapeDtypeStruct(subgrid.shape, subgrid.dtype),
        ),
        in_specs=[vmem] * 2,
        out_specs=(anywhere, anywhere),
        scratch_shapes=[dma((2,))],
    )(residual, subgrid)
    return residual, subgrid[None]


def solution(mesh):
    return jax.shard_map(
        functools.partial(local, mesh.shape["dir"], mesh.shape["tb"]),
        mesh=mesh,
        in_specs=(
            P("tb", None),
            P(None, "tb"),
            P(None, "dir"),
            P(None, "dir", None),
            P(),
            P("dir"),
            P("dir"),
            P("tb", None),
        ),
        out_specs=(P("tb", None), P("tb", None, "dir", None)),
        check_vma=False,
    )
```
